32 devices in a mesh: zone: 4 (over y, x), dev: 8 (over z, core).
Axes of the slice: x: 2, y: 2, z: 4, core: 2. Of those that a mesh axis runs over, the one named last changes fastest.
Arguments:
- quad_weight: float32 [16384, 128], P(('zone', 'dev')), may hold values from 0.002 to 0.014
- param_coords: float32 [16384, 4, 128], P(('zone', 'dev')), may hold values from -1 to 1
- slave_points: float32 [16384, 3, 128], P(('zone', 'dev')), may hold values from -6 to 6
- slave_normals: float32 [16384, 3, 128], P(('zone', 'dev')), may hold values from -1 to 1, as said below
- block_owner: int32 [16384, 1], P(('zone', 'dev')), may hold values from 0 to 7; in each aligned block of 128 rows (0 to 127, 128 to 255, ...) at most 16 rows name the same one
- block_patch: int32 [16384], P(('zone', 'dev')), may hold values from 0 to 8191
- block_count: int32 [32, 4], P(('zone', 'dev')), may hold values from 1 to 128, as said below
- active_flags: int32 [4, 16384], P(None, ('zone', 'dev')), may hold values 0 or 1
- normal_mult: float32 [4, 16384], P(None, ('zone', 'dev')), may hold values from 0.5 to 4
- tangent_mult: float32 [12, 16384], P(None, ('zone', 'dev')), may hold values from -6 to 6
- master_patch: float32 [12, 262144], P(None, ('zone', 'dev')), may hold values from -6 to 6
Outputs:
- mortar_d: float32 [16, 16384], P(None, ('zone', 'dev'))
- mortar_m: float32 [16, 16384], P(None, ('zone', 'dev'))
- gap_lin: float32 [48, 16384], P(None, ('zone', 'dev'))
- gap_res: float32 [4, 16384], P(None, ('zone', 'dev'))
- cone_res: float32 [12, 16384], P(None, ('zone', 'dev'))
The draws below stay inside these ranges and needn't reach their ends.
Inputs may be any that keep to these rules, and one draw needn't show every extreme that they name: Device q's live blocks toward group k are the first block_count[q, k] of its 128 slots for k; in every draw each device fills all 128 slots toward one group, the same group for all devices of one dev index. `slave_normals`: every normal has unit length. `block_owner`: in each aligned block of 128 slots (one device toward one group) no owner is named by more than 16 slots.
All inputs are finite; a program needn't handle non-finite values. No bound on the sum of `active_flags` on one device may be relied on, other than what follows from the above.
Results may differ from the reference program's by a relative error of at most 0.0003.
Values sent between devices are 32-bit elements; how exact they have to be, the bound alone decides.
A program may use at most 320 MiB of HBM per device.

```python
import math
import jax
import jax.numpy as jnp
import numpy as np
from jax import lax

QP = 128
CAP = 128
MP_DEV = 8192
BUCKET = 16
GROUPS = 4
OWNERS = 32
SLOTS_DEV = 512
SLOTS = 16384
MP_ZONE = 65536
PATCHES = 262144
N_DEV = 8


def draw_slave_normals(key, part):
    tilt = jax.random.uniform(key, (SLOTS, 2, QP), jnp.float32, -1.0, 1.0)
    length = jnp.sqrt(1.0 + tilt[:, 0] * tilt[:, 0] + tilt[:, 1] * tilt[:, 1])
    return jnp.stack([tilt[:, 0] / length, tilt[:, 1] / length, 1.0 / length], axis=1)


def draw_block_count(key, part):
    base = jax.random.randint(jax.random.fold_in(key, 11), (OWNERS, GROUPS), 1, CAP + 1)
    owner_index = jnp.arange(OWNERS, dtype=jnp.int32) % N_DEV
    full = jnp.arange(GROUPS, dtype=jnp.int32)[None, :] == (owner_index % GROUPS)[:, None]
    return jnp.where(full, CAP, base).astype(jnp.int32)


def touch_ends(entries, own_key, low, top_value):
    dims = entries.shape
    spot = [jax.random.randint(jax.random.fold_in(own_key, axis), (), 0, dims[axis]) for axis in range(len(dims))]
    entries = entries.at[tuple(spot)].set(low)
    longest = dims.index(max(dims))
    spot[longest] = (spot[longest] + 1) % dims[longest]
    return entries.at[tuple(spot)].set(top_value)


def block_levels(key, extent, split, smallest, high):
    factor_of, own = 1.0, jax.random.fold_in(key, 6)
    for axis_at, blocks in split:
        steps = jnp.exp(jax.random.uniform(jax.random.fold_in(own, axis_at), (blocks,), jnp.float32, smallest / len(split), high / len(split)))
        factor_of = factor_of * jnp.repeat(steps, extent[axis_at] // blocks).reshape([-1 if axis == axis_at else 1 for axis in range(len(extent))])
    return factor_of


def routed_block(key, own, number, rows, count, top, bound, slope):
    sequence = jax.random.permutation(key, count)
    packed, ordinary = shares(count, rows * top, bound, slope, True), shares(count, rows * top, bound, slope, False)
    places = jnp.arange(count)

    def named(sizes, offset_by):
        used = int((sizes > 0).sum())
        fixed = max(1, used // 4)
        moved = fixed + (places - fixed + offset_by * (used - fixed)) % max(1, count - fixed)
        return jnp.zeros((count,), jnp.int32).at[sequence[jnp.where(places < fixed, places, moved)]].set(jnp.asarray(sizes, jnp.int32))

    sizes = jnp.where(number % 4 == 0, named(packed, number // 4), named(ordinary, number - number // 4 - 1))
    mixed = jax.random.permutation(jax.random.fold_in(own, 3), count)
    source_of, receiver = mixed[0:count // 2 * 2:2], mixed[1:count // 2 * 2:2]
    slack = jnp.minimum(sizes[source_of] - 1, bound - sizes[receiver]) // 2
    slack = jnp.where((source_of == sequence[0]) | (receiver == sequence[0]) | (sizes[receiver] == 0), 0, jnp.maximum(slack, 0))
    moved = jax.random.randint(jax.random.fold_in(own, 4), (count // 2,), 0, 1 << 20) % (slack + 1)
    sizes = sizes.at[source_of].add(-moved).at[receiver].add(moved)
    labels = jnp.searchsorted(jnp.cumsum(sizes), jnp.arange(rows * top), side="right").astype(jnp.int32)
    listing = labels.reshape(top, rows).T
    listing = listing[jax.random.permutation(jax.random.fold_in(own, 1), rows)]
    offset_by = jax.random.randint(jax.random.fold_in(own, 2), (rows, 1), 0, top)
    return jnp.take_along_axis(listing, (jnp.arange(top)[None, :] + offset_by) % top, axis=1)


def shares(number_of, total, most, slope, full):
    weights = [(1 << 20) // math.isqrt(grade ** slope) + 1 for grade in range(1, number_of + 1)]
    largest = most if full else min(most, max(-(-total // number_of), total * weights[0] // sum(weights)))
    least = 1 if total - largest >= number_of - 1 else 0
    given, rest = [largest] + [least] * (number_of - 1), total - largest - least * (number_of - 1)
    while rest > 0:
        movable = [i for i in range(1, number_of) if given[i] < largest] or [i for i in range(1, number_of) if given[i] < most]
        pool, budget = sum([weights[i] for i in movable]), rest
        for i in movable:
            addition = min(most - given[i], max(1, budget * weights[i] // pool), rest)
            given[i] = given[i] + addition
            rest = rest - addition
    return np.array(given)


def centred(rng, dims, width, bound, cuts=(), held_as=jnp.bfloat16):
    factor_of = block_levels(rng, dims, cuts, -0.22, 0.18) if cuts else 1.0
    entries = jax.random.normal(rng, dims, jnp.float32) * width * factor_of
    return jnp.minimum(jnp.maximum(entries, -bound), bound).astype(held_as)


def setup_inputs(seed: int = 0) -> dict:
    seeds = jax.random.split(jax.random.key(seed), 12)
    quad_weight = jnp.clip(jnp.exp(math.log(0.014) - 1.9459101 * jax.random.uniform(seeds[0], (SLOTS, QP), jnp.float32) ** block_levels(seeds[0], (SLOTS, QP), ((0, 32),), -0.2, 0.2)), 0.002, 0.014)
    param_coords = jnp.clip(jax.random.uniform(seeds[1], (SLOTS, 4, QP), jnp.float32, -1.0, 1.0) * block_levels(seeds[1], (SLOTS, 4, QP), ((0, 32),), -0.4, 0.0), -1.0, 1.0)
    slave_points = centred(seeds[2], (SLOTS, 3, QP), 1.0, 6.0, ((0, 32),), jnp.float32)
    slave_normals = draw_slave_normals(jax.random.fold_in(seeds[11], 71), 0)
    block_owner_keys = jax.random.split(jax.random.fold_in(seeds[4], 1), SLOTS // CAP)
    block_owner_turns = jax.random.permutation(jax.random.fold_in(seeds[4], 3), SLOTS // CAP)
    block_owner = jax.vmap(lambda own, number: routed_block(jax.random.fold_in(seeds[4], 2), own, number, CAP, N_DEV, 1, BUCKET, 2))(block_owner_keys, block_owner_turns).reshape((SLOTS, 1))
    block_patch = touch_ends(jax.random.randint(seeds[5], (SLOTS,), 0, MP_DEV), jax.random.fold_in(seeds[5], 1), 0, MP_DEV - 1).astype(jnp.int32)
    block_count = draw_block_count(jax.random.fold_in(seeds[11], 71), 0)
    active_flags = touch_ends((jax.random.randint(seeds[7], (4, SLOTS), 0, 3) < 2).astype(jnp.int32), jax.random.fold_in(seeds[7], 1), 0, 1)
    normal_mult = jnp.clip(jnp.exp(math.log(4.0) - 2.0794415 * jax.random.uniform(seeds[8], (4, SLOTS), jnp.float32) ** block_levels(seeds[8], (4, SLOTS), ((1, 32),), -0.2, 0.2)), 0.5, 4.0)
    tangent_mult = centred(seeds[9], (12, SLOTS), 1.0, 6.0, ((1, 32),), jnp.float32)
    master_patch = centred(seeds[10], (12, PATCHES), 1.0, 6.0, ((1, 32),), jnp.float32)
    return dict(quad_weight=quad_weight, param_coords=param_coords, slave_points=slave_points, slave_normals=slave_normals, block_owner=block_owner, block_patch=block_patch, block_count=block_count, active_flags=active_flags, normal_mult=normal_mult, tangent_mult=tangent_mult, master_patch=master_patch)


friction_coef = 0.3
newton_scale = 4.0

def bilinear(first, second):
    return jnp.stack([0.25 * (1.0 - first) * (1.0 - second), 0.25 * (1.0 + first) * (1.0 - second), 0.25 * (1.0 + first) * (1.0 + second), 0.25 * (1.0 - first) * (1.0 + second)], axis=0)

def slave_terms(weight, coords):
    shape_s = bilinear(coords[:, 2], coords[:, 3])
    weighted = weight[None] * shape_s
    return lax.optimization_barrier(jnp.sum(weighted[:, None] * shape_s[None], axis=-1)).reshape(16, -1)

def master_terms(weight, coords, points, normals, corners):
    shape_s = bilinear(coords[:, 2], coords[:, 3])
    shape_m = bilinear(coords[:, 0], coords[:, 1])
    weighted = weight[None] * shape_s
    paired = weighted[:, None] * shape_m[None]
    mortar_m = lax.optimization_barrier(jnp.sum(paired, axis=-1)).reshape(16, -1)
    diffs = []
    for direction in range(3):
        position = lax.optimization_barrier(jnp.sum(shape_m * corners[4 * direction:4 * direction + 4][:, :, None], axis=0))
        diffs.append(position - points[:, direction])
    gap_point = normals[:, 0] * diffs[0] + normals[:, 1] * diffs[1] + normals[:, 2] * diffs[2]
    wgap = lax.optimization_barrier(jnp.sum(weighted * gap_point[None], axis=-1))
    slips = [lax.optimization_barrier(jnp.sum(weighted * (diffs[direction] - normals[:, direction] * gap_point)[None], axis=-1)) for direction in range(3)]
    lins = [lax.optimization_barrier(jnp.sum(paired * normals[:, direction][None, None], axis=-1)).reshape(16, -1) for direction in range(3)]
    return (mortar_m, wgap, jnp.concatenate(slips, axis=0), jnp.concatenate(lins, axis=0))

def residuals(wgap, wslip, active, normal_mult, tangent_mult):
    radius = friction_coef * normal_mult
    trial = tangent_mult + newton_scale * wslip
    length = jnp.sqrt(trial[0:4] * trial[0:4] + trial[4:8] * trial[4:8] + trial[8:12] * trial[8:12])
    factor = radius / jnp.maximum(radius, length)
    factor_all = jnp.concatenate([factor, factor, factor], axis=0)
    active_all = jnp.concatenate([active, active, active], axis=0)
    cone = jnp.where(active_all == 1, tangent_mult - factor_all * trial, tangent_mult)
    gap = jnp.where(active == 1, wgap, normal_mult)
    return (gap, cone)

def live_slots(counts, slots, groups):
    cap = slots // groups
    index = jnp.arange(slots, dtype=jnp.int32)
    group_of = index // cap
    per_slot = lax.optimization_barrier(jnp.sum(jnp.where(group_of[:, None] == jnp.arange(groups, dtype=jnp.int32)[None, :], counts[None, :], 0), axis=1))
    return index % cap < per_slot

def reference(quad_weight, param_coords, slave_points, slave_normals, block_owner, block_patch, block_count, active_flags, normal_mult, tangent_mult, master_patch):

    def per_owner(pieces):
        weight, coords, points, normals, owner_ids, patch_ids, counts, active, nmult, tmult = pieces
        slots = weight.shape[0]
        cap = slots // GROUPS
        group_of = jnp.arange(slots, dtype=jnp.int32) // cap
        global_ids = (group_of * MP_ZONE + owner_ids * MP_DEV + patch_ids).astype(jnp.int32)
        corners = jnp.take(master_patch, global_ids, axis=1)
        mortar_d = slave_terms(weight, coords)
        mortar_m, wgap, wslip, gap_lin = master_terms(weight, coords, points, normals, corners)
        gap, cone = residuals(wgap, wslip, active, nmult, tmult)
        live = live_slots(counts, slots, GROUPS)[None]
        return (jnp.where(live, mortar_d, 0.0), jnp.where(live, mortar_m, 0.0), jnp.where(live, gap_lin, 0.0), jnp.where(live, gap, 0.0), jnp.where(live, cone, 0.0))

    def by_owner(array, rows):
        return array.reshape(rows, OWNERS, SLOTS_DEV).transpose(1, 0, 2)
    pieces = (quad_weight.reshape(OWNERS, SLOTS_DEV, QP), param_coords.reshape(OWNERS, SLOTS_DEV, 4, QP), slave_points.reshape(OWNERS, SLOTS_DEV, 3, QP), slave_normals.reshape(OWNERS, SLOTS_DEV, 3, QP), block_owner.reshape(OWNERS, SLOTS_DEV), block_patch.reshape(OWNERS, SLOTS_DEV), block_count, by_owner(active_flags, 4), by_owner(normal_mult, 4), by_owner(tangent_mult, 12))
    results = lax.map(per_owner, pieces)

    def joined(array):
        return array.transpose(1, 0, 2).reshape(array.shape[1], OWNERS * SLOTS_DEV)
    return (joined(results[0]), joined(results[1]), joined(results[2]), joined(results[3]), joined(results[4]))
```

```python
import jax
import jax.numpy as jnp
from jax import lax
from jax.sharding import PartitionSpec as P

BUCKET = 16


friction_coef = 0.3
newton_scale = 4.0


def bilinear(first, second):
    return jnp.stack(
        [
            0.25 * (1.0 - first) * (1.0 - second),
            0.25 * (1.0 + first) * (1.0 - second),
            0.25 * (1.0 + first) * (1.0 + second),
            0.25 * (1.0 - first) * (1.0 + second),
        ],
        axis=0,
    )


def slave_terms(weight, coords):
    shape_s = bilinear(coords[:, 2], coords[:, 3])
    weighted = weight[None] * shape_s
    return jnp.sum(weighted[:, None] * shape_s[None], axis=-1).reshape(16, -1)


def master_terms(weight, coords, points, normals, corners):
    shape_s = bilinear(coords[:, 2], coords[:, 3])
    shape_m = bilinear(coords[:, 0], coords[:, 1])
    weighted = weight[None] * shape_s
    paired = weighted[:, None] * shape_m[None]
    mortar_m = jnp.sum(paired, axis=-1).reshape(16, -1)
    diffs = []
    for direction in range(3):
        position = jnp.sum(shape_m * corners[4 * direction : 4 * direction + 4][:, :, None], axis=0)
        diffs.append(position - points[:, direction])
    gap_point = normals[:, 0] * diffs[0] + normals[:, 1] * diffs[1] + normals[:, 2] * diffs[2]
    wgap = jnp.sum(weighted * gap_point[None], axis=-1)
    slips = [
        jnp.sum(weighted * (diffs[direction] - normals[:, direction] * gap_point)[None], axis=-1)
        for direction in range(3)
    ]
    lins = [
        jnp.sum(paired * normals[:, direction][None, None], axis=-1).reshape(16, -1)
        for direction in range(3)
    ]
    return (mortar_m, wgap, jnp.concatenate(slips, axis=0), jnp.concatenate(lins, axis=0))


def residuals(wgap, wslip, active, normal_mult, tangent_mult):
    radius = friction_coef * normal_mult
    trial = tangent_mult + newton_scale * wslip
    length = jnp.sqrt(trial[0:4] * trial[0:4] + trial[4:8] * trial[4:8] + trial[8:12] * trial[8:12])
    factor = radius / jnp.maximum(radius, length)
    factor_all = jnp.concatenate([factor, factor, factor], axis=0)
    active_all = jnp.concatenate([active, active, active], axis=0)
    cone = jnp.where(active_all == 1, tangent_mult - factor_all * trial, tangent_mult)
    gap = jnp.where(active == 1, wgap, normal_mult)
    return (gap, cone)


def live_slots(counts, slots, groups):
    cap = slots // groups
    index = jnp.arange(slots, dtype=jnp.int32)
    group_of = index // cap
    per_slot = jnp.sum(
        jnp.where(
            group_of[:, None] == jnp.arange(groups, dtype=jnp.int32)[None, :], counts[None, :], 0
        ),
        axis=1,
    )
    return index % cap < per_slot


def lookup(owner, patch, master_patch):
    count = owner.shape[0]
    peers = lax.axis_size("dev")
    zones = lax.axis_size("zone")
    block = count // zones
    width = peers * BUCKET
    owner = owner.reshape(zones, block)
    patch = patch.reshape(zones, block)
    index = jnp.arange(block, dtype=jnp.int32)
    earlier = index[:, None] < index[None, :]
    same = (owner[:, :, None] == owner[:, None, :]) & earlier[None]
    rank = jnp.sum(same.astype(jnp.int32), axis=1)
    place = owner * BUCKET + rank
    chosen = place[:, :, None] == jnp.arange(width, dtype=jnp.int32)[None, None, :]
    table = jnp.sum(jnp.where(chosen, patch[:, :, None], 0), axis=1)
    asked = lax.all_to_all(
        table.reshape(zones * peers, BUCKET), ("zone", "dev"), split_axis=0, concat_axis=0, tiled=True
    )
    found = jnp.take(master_patch.T, asked.reshape(-1), axis=0, mode="clip")
    replies = lax.all_to_all(
        found.reshape(zones * peers, BUCKET * 12), ("zone", "dev"), split_axis=0, concat_axis=0, tiled=True
    )
    rows = replies.reshape(zones, width, 12)
    corners = lax.dot_general(
        rows,
        chosen.astype(jnp.float32),
        (((1,), (2,)), ((0,), (0,))),
        precision=lax.Precision.HIGHEST,
    )
    return corners.transpose(1, 0, 2).reshape(12, count)


def local(
    quad_weight,
    param_coords,
    slave_points,
    slave_normals,
    block_owner,
    block_patch,
    block_count,
    active_flags,
    normal_mult,
    tangent_mult,
    master_patch,
):
    groups = lax.axis_size("zone")
    slots = quad_weight.shape[0]
    mortar_d = slave_terms(quad_weight, param_coords)
    owner_ids = block_owner[:, 0]
    corners = lookup(owner_ids, block_patch, master_patch)
    back_m, back_gap, back_slip, back_lin = master_terms(
        quad_weight, param_coords, slave_points, slave_normals, corners
    )
    gap, cone = residuals(back_gap, back_slip, active_flags, normal_mult, tangent_mult)
    live = live_slots(block_count[0], slots, groups)[None]
    return (
        jnp.where(live, mortar_d, 0.0),
        jnp.where(live, back_m, 0.0),
        jnp.where(live, back_lin, 0.0),
        jnp.where(live, gap, 0.0),
        jnp.where(live, cone, 0.0),
    )


def solution(mesh):
    placed = (
        P(("zone", "dev"), None),
        P(("zone", "dev"), None, None),
        P(("zone", "dev"), None, None),
        P(("zone", "dev"), None, None),
        P(("zone", "dev"), None),
        P(("zone", "dev")),
        P(("zone", "dev"), None),
        P(None, ("zone", "dev")),
        P(None, ("zone", "dev")),
        P(None, ("zone", "dev")),
        P(None, ("zone", "dev")),
    )
    return jax.shard_map(
        local,
        mesh=mesh,
        in_specs=placed,
        out_specs=(
            P(None, ("zone", "dev")),
            P(None, ("zone", "dev")),
            P(None, ("zone", "dev")),
            P(None, ("zone", "dev")),
            P(None, ("zone", "dev")),
        ),
        check_vma=False,
    )
```

```python
import functools

import jax
import jax.numpy as jnp
from jax import lax
from jax.experimental import pallas as pl
from jax.experimental.pallas import tpu as pltpu
from jax.sharding import PartitionSpec as P

BUCKET = 16
LANES = 128
MESH = pl.DeviceIdType.MESH

friction_coef = 0.3
newton_scale = 4.0


def pick(values, index, axis):
    return jnp.take_along_axis(values, index, axis=axis, mode="promise_in_bounds")


def iota(shape, axis):
    return lax.broadcasted_iota(jnp.int32, shape, axis)


def bilinear(first, second):
    return (
        0.25 * (1.0 - first) * (1.0 - second),
        0.25 * (1.0 + first) * (1.0 - second),
        0.25 * (1.0 + first) * (1.0 + second),
        0.25 * (1.0 - first) * (1.0 + second),
    )


NS, NM, WS, PT, NV = 0, 4, 8, 12, 15


def kernel(
    zones,
    peers,
    quad_hbm,
    coords_hbm,
    points_hbm,
    normals_hbm,
    master_hbm,
    owner_ref,
    patch_ref,
    count_ref,
    active_ref,
    nmult_ref,
    tmult_ref,
    d_ref,
    m_ref,
    lin_ref,
    gap_ref,
    cone_ref,
    quad,
    coords,
    points,
    normals,
    table,
    packed,
    terms,
    req_out,
    req_in,
    rep_out,
    rep_in,
    load_sem,
    req_send,
    req_recv,
    rep_send,
    rep_recv,
):
    count = zones * peers
    groups = peers // 8
    zone, dev = lax.axis_index("zone"), lax.axis_index("dev")
    me = zone * peers + dev
    tiles = table.shape[1] // LANES
    half = tiles // 2

    loads = [
        pltpu.make_async_copy(source, target, load_sem.at[at])
        for at, (source, target) in enumerate(
            (
                (master_hbm, table),
                (quad_hbm, quad),
                (coords_hbm, coords),
                (points_hbm, points),
                (normals_hbm, normals),
            )
        )
    ]
    for load in loads:
        load.start()

    barrier = pltpu.get_barrier_semaphore()

    def greet(step, carry):
        other = lax.rem(me + step, count)
        pl.semaphore_signal(
            barrier,
            inc=1,
            device_id=(lax.div(other, peers), lax.rem(other, peers)),
            device_id_type=MESH,
        )
        return carry

    lax.fori_loop(1, count, greet, 0)

    sub, lane = iota((8, LANES), 0), iota((8, LANES), 1)
    wide_sub, wide_lane = iota((LANES, LANES), 0), iota((LANES, LANES), 1)
    ranks = []
    for k in range(zones):
        owner = owner_ref[k : k + 1, :].astype(jnp.float32)
        patch = patch_ref[k : k + 1, :].astype(jnp.float32)
        across = jnp.broadcast_to(owner, (LANES, LANES))
        same = (across.T == across) & (wide_sub < wide_lane)
        rank = jnp.sum(jnp.where(same, 1.0, 0.0), axis=0, keepdims=True).astype(jnp.int32)
        ranks.append(rank)
        place = owner_ref[k : k + 1, :] * BUCKET + rank
        for g in range(groups):
            chosen = jnp.where(wide_sub + g * LANES == place, jnp.broadcast_to(patch, (LANES, LANES)), 0.0)
            asked = jnp.sum(chosen.T, axis=0, keepdims=True).astype(jnp.int32)
            rows = pick(jnp.broadcast_to(asked, (8, LANES)), sub * BUCKET + (lane & 15), 1)
            for o in range(8):
                req_out[k * peers + g * 8 + o] = rows[o : o + 1, :]

    pl.semaphore_wait(barrier, count - 1)

    def ask(step, carry):
        other = lax.rem(me + step, count)
        pltpu.make_async_remote_copy(
            src_ref=req_out.at[other],
            dst_ref=req_in.at[me],
            send_sem=req_send,
            recv_sem=req_recv.at[zone],
            device_id=(lax.div(other, peers), lax.rem(other, peers)),
            device_id_type=MESH,
        ).start()
        return carry

    lax.fori_loop(1, count, ask, 0)
    pltpu.make_async_copy(req_out.at[me], req_in.at[me], req_recv.at[zone]).start()

    loads[0].wait()
    packed[0:4, :] = table[8:12, 0 : half * LANES]
    packed[4:8, :] = table[8:12, half * LANES : tiles * LANES]
    for load in loads[1:]:
        load.wait()

    def stage(k, carry):
        rows = pl.ds(pl.multiple_of(k * LANES, LANES), LANES)

        def coord(which):
            return coords[pl.ds(k * (4 * LANES) + which, LANES, stride=4), :].T

        weight = quad[rows, :].T
        shape_s = bilinear(coord(2), coord(3))
        for i in range(4):
            terms[NS + i, k] = shape_s[i]
            terms[WS + i, k] = weight * shape_s[i]
        shape_m = bilinear(coord(0), coord(1))
        for i in range(4):
            terms[NM + i, k] = shape_m[i]
        for c in range(3):
            terms[PT + c, k] = points[c, rows, :].T
            terms[NV + c, k] = normals[c, rows, :].T
        return carry

    lax.fori_loop(0, zones, stage, 0)

    skew = ((lane >> 4) - sub) & 7
    skew_low = ((lane >> 4) - (sub & 3)) & 7
    upper = jnp.where(sub >= 4, half, 0)
    for dz in range(zones):
        target = lax.rem(zone + dz, zones)
        whole = req_in.at[pl.ds(target * peers, peers)]
        pltpu.make_async_copy(whole, whole, req_recv.at[target]).wait()
        for g in range(groups):
            base = target * peers + g * 8
            rows = jnp.concatenate([req_in[base + v] for v in range(8)], axis=0)
            first = pick(rows, skew, 0)
            second = pick(rows, skew_low, 0)
            high, low = first >> 7, first & 127
            high_b, low_b = (second >> 7) - upper, second & 127
            zero = jnp.zeros((8, LANES), jnp.float32)

            def search(h, accs):
                acc, acc_a, acc_b = accs
                at = pl.ds(pl.multiple_of(h * LANES, LANES), LANES)
                later = pl.ds(pl.multiple_of((h + half) * LANES, LANES), LANES)
                acc = jnp.where(high == h, pick(table[0:8, at], low, 1), acc)
                acc_a = jnp.where(high == h + half, pick(table[0:8, later], low, 1), acc_a)
                acc_b = jnp.where(high_b == h, pick(packed[:, at], low_b, 1), acc_b)
                return acc, acc_a, acc_b

            acc, acc_a, acc_b = lax.fori_loop(0, half, search, (zero, zero, zero), unroll=8)
            acc = jnp.where(high >= half, acc_a, acc)
            acc_b = acc_b + pltpu.roll(acc_b, 4, 0)
            out_a, out_b = pick(acc, skew, 0), pick(acc_b, skew, 0)
            for v in range(8):
                rep_out[base + v, :, 0:LANES] = out_a[v : v + 1, :]
                rep_out[base + v, :, LANES : 2 * LANES] = out_b[v : v + 1, :]

        def answer(step, carry):
            peer = lax.rem(dev + step, peers)
            pltpu.make_async_remote_copy(
                src_ref=rep_out.at[target * peers + peer],
                dst_ref=rep_in.at[me],
                send_sem=rep_send,
                recv_sem=rep_recv.at[zone],
                device_id=(target, peer),
                device_id_type=MESH,
            ).start()
            return carry

        if dz == 0:
            pltpu.make_async_copy(rep_out.at[me], rep_in.at[me], rep_recv.at[zone]).start()
        lax.fori_loop(1 if dz == 0 else 0, peers, answer, 0)

    for k in range(zones):
        live = lane[0:1] < count_ref[0, k]
        cols = slice(k * LANES, (k + 1) * LANES)

        def keep(ref, row, value):
            total = jnp.sum(value, axis=0, keepdims=True)
            ref[row : row + 1, cols] = jnp.where(live, total, 0.0)

        for i in range(4):

            def add(t, accs):
                at = pl.ds(pl.multiple_of(t * 8, 8), 8)
                weighted = terms[WS + i, k, at, :]
                normal = [terms[NV + c, k, at, :] for c in range(3)]
                out = [accs[j] + weighted * terms[NS + j, k, at, :] for j in range(4)]
                pairs = [weighted * terms[NM + a, k, at, :] for a in range(4)]
                out += [accs[4 + a] + pairs[a] for a in range(4)]
                out += [accs[8 + c * 4 + a] + pairs[a] * normal[c] for c in range(3) for a in range(4)]
                return tuple(out)

            zero = jnp.zeros((8, LANES), jnp.float32)
            accs = lax.fori_loop(0, LANES // 8, add, (zero,) * 20, unroll=4)
            for j in range(4):
                keep(d_ref, i * 4 + j, accs[j])
                keep(m_ref, i * 4 + j, accs[4 + j])
                for c in range(3):
                    keep(lin_ref, c * 16 + i * 4 + j, accs[8 + c * 4 + j])

    turn = dev & 7
    undo = ((((lane >> 4) - sub) & 7) << 4) + (lane & 15)
    mix = ((lane >> 4) - sub - turn) & 7
    for dz in range(zones):
        k = dz
        whole = rep_in.at[pl.ds(k * peers, peers)]
        pltpu.make_async_copy(whole, whole, rep_recv.at[k]).wait()
        owner = jnp.broadcast_to(owner_ref[k : k + 1, :], (8, LANES))
        seat = (((owner + sub + turn) & 7) << 4) + jnp.broadcast_to(ranks[k], (8, LANES))
        found = []
        for h in range(2):
            total = jnp.zeros((8, LANES), jnp.float32)
            for g in range(groups):
                rows = jnp.concatenate(
                    [
                        rep_in[k * peers + g * 8 + o, :, h * LANES : (h + 1) * LANES]
                        for o in range(8)
                    ],
                    axis=0,
                )
                rows = pick(pick(pick(rows, undo, 1), mix, 0), seat, 1)
                total = jnp.where((owner >> 3) == g, rows, total)
            found.append(total)
        corner = [
            jnp.broadcast_to(found[r // 8][r % 8 : r % 8 + 1, :], (8, LANES)) for r in range(12)
        ]

        def add(t, accs):
            at = pl.ds(pl.multiple_of(t * 8, 8), 8)
            shape_m = [terms[NM + a, k, at, :] for a in range(4)]
            diff, normal = [], [terms[NV + c, k, at, :] for c in range(3)]
            for c in range(3):
                position = shape_m[0] * corner[4 * c]
                for a in range(1, 4):
                    position = position + shape_m[a] * corner[4 * c + a]
                diff.append(position - terms[PT + c, k, at, :])
            gap = normal[0] * diff[0] + normal[1] * diff[1] + normal[2] * diff[2]
            slip = [diff[c] - normal[c] * gap for c in range(3)]
            weighted = [terms[WS + i, k, at, :] for i in range(4)]
            out = [accs[i] + weighted[i] * gap for i in range(4)]
            out += [accs[4 + c * 4 + i] + weighted[i] * slip[c] for c in range(3) for i in range(4)]
            return tuple(out)

        zero = jnp.zeros((8, LANES), jnp.float32)
        accs = lax.fori_loop(0, LANES // 8, add, (zero,) * 16, unroll=2)
        sums = [jnp.sum(acc, axis=0, keepdims=True) for acc in accs]
        cols = slice(k * LANES, (k + 1) * LANES)
        live = lane[0:1] < count_ref[0, k]
        wgap = jnp.concatenate(sums[0:4], axis=0)
        active = active_ref[:, cols] == 1
        normal = nmult_ref[:, cols]
        tangent = [tmult_ref[4 * c : 4 * c + 4, cols] for c in range(3)]
        trial = [
            tangent[c] + newton_scale * jnp.concatenate(sums[4 + 4 * c : 8 + 4 * c], axis=0)
            for c in range(3)
        ]
        radius = friction_coef * normal
        length = jnp.sqrt(trial[0] * trial[0] + trial[1] * trial[1] + trial[2] * trial[2])
        factor = radius / jnp.maximum(radius, length)
        for c in range(3):
            cone = jnp.where(active, tangent[c] - factor * trial[c], tangent[c])
            cone_ref[4 * c : 4 * c + 4, cols] = jnp.where(live, cone, 0.0)
        gap_ref[:, cols] = jnp.where(live, jnp.where(active, wgap, normal), 0.0)

    sent = req_out.at[pl.ds(0, count - 1)]
    pltpu.make_async_copy(sent, sent, req_send).wait()
    sent = rep_out.at[pl.ds(0, count - 1)]
    pltpu.make_async_copy(sent, sent, rep_send).wait()


def local(
    quad_weight,
    param_coords,
    slave_points,
    slave_normals,
    block_owner,
    block_patch,
    block_count,
    active_flags,
    normal_mult,
    tangent_mult,
    master_patch,
):
    zones, peers = lax.axis_size("zone"), lax.axis_size("dev")
    slots, gauss = quad_weight.shape
    block = slots // zones
    patches = master_patch.shape[1]
    count = zones * peers
    f32 = jnp.float32
    anywhere = pl.BlockSpec(memory_space=pl.ANY)
    vmem = pl.BlockSpec(memory_space=pltpu.VMEM)
    smem = pl.BlockSpec(memory_space=pltpu.SMEM)
    out = [jax.ShapeDtypeStruct((rows, slots), f32) for rows in (16, 16, 48, 4, 12)]
    return pl.pallas_call(
        functools.partial(kernel, zones, peers),
        out_shape=out,
        in_specs=[anywhere] * 5 + [vmem, vmem, smem, vmem, vmem, vmem],
        out_specs=[vmem] * 5,
        scratch_shapes=[
            pltpu.VMEM((slots, gauss), f32),
            pltpu.VMEM((4 * slots, gauss), f32),
            pltpu.VMEM((3, slots, gauss), f32),
            pltpu.VMEM((3, slots, gauss), f32),
            pltpu.VMEM((12, patches), f32),
            pltpu.VMEM((8, patches // 2), f32),
            pltpu.VMEM((18, zones, gauss, block), f32),
            pltpu.VMEM((count, 1, LANES), jnp.int32),
            pltpu.VMEM((count, 1, LANES), jnp.int32),
            pltpu.VMEM((count, 1, 2 * LANES), f32),
            pltpu.VMEM((count, 1, 2 * LANES), f32),
            pltpu.SemaphoreType.DMA((5,)),
            pltpu.SemaphoreType.DMA,
            pltpu.SemaphoreType.DMA((zones,)),
            pltpu.SemaphoreType.DMA,
            pltpu.SemaphoreType.DMA((zones,)),
        ],
        compiler_params=pltpu.CompilerParams(
            collective_id=0, has_side_effects=True, vmem_limit_bytes=40 * 2**20
        ),
    )(
        quad_weight,
        param_coords.reshape(4 * slots, gauss),
        slave_points.transpose(1, 0, 2),
        slave_normals.transpose(1, 0, 2),
        master_patch,
        block_owner.reshape(zones, block),
        block_patch.reshape(zones, block),
        block_count,
        active_flags,
        normal_mult,
        tangent_mult,
    )


def solution(mesh):
    rows = P(("zone", "dev"))
    columns = P(None, ("zone", "dev"))
    return jax.shard_map(
        local,
        mesh=mesh,
        in_specs=(rows,) * 7 + (columns,) * 4,
        out_specs=(columns,) * 5,
        check_vma=False,
    )
```

```python
import functools

import jax
import jax.numpy as jnp
from jax import lax
from jax.experimental import pallas as pl
from jax.experimental.pallas import tpu as pltpu
from jax.sharding import PartitionSpec as P

BUCKET = 16
LANES = 128
MESH = pl.DeviceIdType.MESH

friction_coef = 0.3
newton_scale = 4.0


def pick(values, index, axis):
    return jnp.take_along_axis(values, index, axis=axis, mode="promise_in_bounds")


def iota(shape, axis):
    return lax.broadcasted_iota(jnp.int32, shape, axis)


def bilinear(first, second):
    return (
        0.25 * (1.0 - first) * (1.0 - second),
        0.25 * (1.0 + first) * (1.0 - second),
        0.25 * (1.0 + first) * (1.0 + second),
        0.25 * (1.0 - first) * (1.0 + second),
    )


NS, NM, WS, PT, NV = 0, 4, 8, 12, 15


def kernel(
    zones,
    peers,
    quad_hbm,
    coords_hbm,
    points_hbm,
    normals_hbm,
    master_hbm,
    owner_hbm,
    patch_hbm,
    count_hbm,
    active_hbm,
    nmult_hbm,
    tmult_hbm,
    d_ref,
    m_ref,
    lin_ref,
    gap_ref,
    cone_ref,
    quad,
    coords,
    points,
    normals,
    table,
    packed,
    owner_ref,
    patch_ref,
    count_ref,
    active_ref,
    nmult_ref,
    tmult_ref,
    terms,
    req_out,
    req_in,
    rep_out,
    rep_in,
    load_sem,
    req_send,
    req_recv,
    rep_send,
    rep_recv,
):
    count = zones * peers
    groups = peers // 8
    zone, dev = lax.axis_index("zone"), lax.axis_index("dev")
    me = zone * peers + dev
    tiles = table.shape[1] // LANES
    half = tiles // 2

    loads = [
        pltpu.make_async_copy(source, target, load_sem.at[at])
        for at, (source, target) in enumerate(
            (
                (owner_hbm, owner_ref),
                (patch_hbm, patch_ref),
                (master_hbm, table),
                (quad_hbm, quad),
                (coords_hbm, coords),
                (points_hbm, points),
                (normals_hbm, normals),
                (count_hbm, count_ref),
                (active_hbm, active_ref),
                (nmult_hbm, nmult_ref),
                (tmult_hbm, tmult_ref),
            )
        )
    ]
    for load in loads:
        load.start()

    barrier = pltpu.get_barrier_semaphore()

    def greet(step, carry):
        other = lax.rem(me + step, count)
        pl.semaphore_signal(
            barrier,
            inc=1,
            device_id=(lax.div(other, peers), lax.rem(other, peers)),
            device_id_type=MESH,
        )
        return carry

    lax.fori_loop(1, count, greet, 0)

    sub, lane = iota((8, LANES), 0), iota((8, LANES), 1)
    wide_sub, wide_lane = iota((LANES, LANES), 0), iota((LANES, LANES), 1)
    ranks = []
    loads[0].wait()
    loads[1].wait()
    for k in range(zones):
        owner = owner_ref[k : k + 1, :].astype(jnp.float32)
        patch = patch_ref[k : k + 1, :].astype(jnp.float32)
        across = jnp.broadcast_to(owner, (LANES, LANES))
        same = (across.T == across) & (wide_sub < wide_lane)
        rank = jnp.sum(jnp.where(same, 1.0, 0.0), axis=0, keepdims=True).astype(jnp.int32)
        ranks.append(rank)
        place = owner_ref[k : k + 1, :] * BUCKET + rank
        for g in range(groups):
            chosen = jnp.where(wide_sub + g * LANES == place, jnp.broadcast_to(patch, (LANES, LANES)), 0.0)
            asked = jnp.sum(chosen.T, axis=0, keepdims=True).astype(jnp.int32)
            rows = pick(jnp.broadcast_to(asked, (8, LANES)), sub * BUCKET + (lane & 15), 1)
            for o in range(8):
                req_out[k * peers + g * 8 + o] = rows[o : o + 1, :]

    pl.semaphore_wait(barrier, count - 1)

    def ask(step, carry):
        other = lax.rem(me + step, count)
        pltpu.make_async_remote_copy(
            src_ref=req_out.at[other],
            dst_ref=req_in.at[me],
            send_sem=req_send,
            recv_sem=req_recv.at[zone],
            device_id=(lax.div(other, peers), lax.rem(other, peers)),
            device_id_type=MESH,
        ).start()
        return carry

    lax.fori_loop(1, count, ask, 0)
    pltpu.make_async_copy(req_out.at[me], req_in.at[me], req_recv.at[zone]).start()

    loads[2].wait()
    packed[0:4, :] = table[8:12, 0 : half * LANES]
    packed[4:8, :] = table[8:12, half * LANES : tiles * LANES]
    for load in loads[3:]:
        load.wait()

    def stage(k, carry):
        rows = pl.ds(pl.multiple_of(k * LANES, LANES), LANES)

        def coord(which):
            return coords[pl.ds(k * (4 * LANES) + which, LANES, stride=4), :].T

        weight = quad[rows, :].T
        shape_s = bilinear(coord(2), coord(3))
        for i in range(4):
            terms[NS + i, k] = shape_s[i]
            terms[WS + i, k] = weight * shape_s[i]
        shape_m = bilinear(coord(0), coord(1))
        for i in range(4):
            terms[NM + i, k] = shape_m[i]
        for c in range(3):
            terms[PT + c, k] = points[c, rows, :].T
            terms[NV + c, k] = normals[c, rows, :].T
        return carry

    lax.fori_loop(0, zones, stage, 0)

    skew = ((lane >> 4) - sub) & 7
    skew_low = ((lane >> 4) - (sub & 3)) & 7
    upper = jnp.where(sub >= 4, half, 0)
    for dz in range(zones):
        target = lax.rem(zone + dz, zones)
        whole = req_in.at[pl.ds(target * peers, peers)]
        pltpu.make_async_copy(whole, whole, req_recv.at[target]).wait()
        for g in range(groups):
            base = target * peers + g * 8
            rows = jnp.concatenate([req_in[base + v] for v in range(8)], axis=0)
            first = pick(rows, skew, 0)
            second = pick(rows, skew_low, 0)
            high, low = first >> 7, first & 127
            high_b, low_b = (second >> 7) - upper, second & 127
            zero = jnp.zeros((8, LANES), jnp.float32)

            def search(h, accs):
                acc, acc_a, acc_b = accs
                at = pl.ds(pl.multiple_of(h * LANES, LANES), LANES)
                later = pl.ds(pl.multiple_of((h + half) * LANES, LANES), LANES)
                acc = jnp.where(high == h, pick(table[0:8, at], low, 1), acc)
                acc_a = jnp.where(high == h + half, pick(table[0:8, later], low, 1), acc_a)
                acc_b = jnp.where(high_b == h, pick(packed[:, at], low_b, 1), acc_b)
                return acc, acc_a, acc_b

            acc, acc_a, acc_b = lax.fori_loop(0, half, search, (zero, zero, zero), unroll=8)
            acc = jnp.where(high >= half, acc_a, acc)
            acc_b = acc_b + pltpu.roll(acc_b, 4, 0)
            out_a, out_b = pick(acc, skew, 0), pick(acc_b, skew, 0)
            for v in range(8):
                rep_out[base + v, :, 0:LANES] = out_a[v : v + 1, :]
                rep_out[base + v, :, LANES : 2 * LANES] = out_b[v : v + 1, :]

        def answer(step, carry):
            peer = lax.rem(dev + step, peers)
            pltpu.make_async_remote_copy(
                src_ref=rep_out.at[target * peers + peer],
                dst_ref=rep_in.at[me],
                send_sem=rep_send,
                recv_sem=rep_recv.at[zone],
                device_id=(target, peer),
                device_id_type=MESH,
            ).start()
            return carry

        if dz == 0:
            pltpu.make_async_copy(rep_out.at[me], rep_in.at[me], rep_recv.at[zone]).start()
        lax.fori_loop(1 if dz == 0 else 0, peers, answer, 0)

    for k in range(zones):
        live = lane[0:1] < count_ref[0:1, k : k + 1]
        cols = slice(k * LANES, (k + 1) * LANES)

        def keep(ref, row, value):
            total = jnp.sum(value, axis=0, keepdims=True)
            ref[row : row + 1, cols] = jnp.where(live, total, 0.0)

        for i in range(4):

            def add(t, accs):
                at = pl.ds(pl.multiple_of(t * 8, 8), 8)
                weighted = terms[WS + i, k, at, :]
                normal = [terms[NV + c, k, at, :] for c in range(3)]
                out = [accs[j] + weighted * terms[NS + j, k, at, :] for j in range(4)]
                pairs = [weighted * terms[NM + a, k, at, :] for a in range(4)]
                out += [accs[4 + a] + pairs[a] for a in range(4)]
                out += [accs[8 + c * 4 + a] + pairs[a] * normal[c] for c in range(3) for a in range(4)]
                return tuple(out)

            zero = jnp.zeros((8, LANES), jnp.float32)
            accs = lax.fori_loop(0, LANES // 8, add, (zero,) * 20, unroll=4)
            for j in range(4):
                keep(d_ref, i * 4 + j, accs[j])
                keep(m_ref, i * 4 + j, accs[4 + j])
                for c in range(3):
                    keep(lin_ref, c * 16 + i * 4 + j, accs[8 + c * 4 + j])

    turn = dev & 7
    undo = ((((lane >> 4) - sub) & 7) << 4) + (lane & 15)
    mix = ((lane >> 4) - sub - turn) & 7
    for dz in range(zones):
        k = dz
        whole = rep_in.at[pl.ds(k * peers, peers)]
        pltpu.make_async_copy(whole, whole, rep_recv.at[k]).wait()
        owner = jnp.broadcast_to(owner_ref[k : k + 1, :], (8, LANES))
        seat = (((owner + sub + turn) & 7) << 4) + jnp.broadcast_to(ranks[k], (8, LANES))
        found = []
        for h in range(2):
            total = jnp.zeros((8, LANES), jnp.float32)
            for g in range(groups):
                rows = jnp.concatenate(
                    [
                        rep_in[k * peers + g * 8 + o, :, h * LANES : (h + 1) * LANES]
                        for o in range(8)
                    ],
                    axis=0,
                )
                rows = pick(pick(pick(rows, undo, 1), mix, 0), seat, 1)
                total = jnp.where((owner >> 3) == g, rows, total)
            found.append(total)
        corner = [
            jnp.broadcast_to(found[r // 8][r % 8 : r % 8 + 1, :], (8, LANES)) for r in range(12)
        ]

        def add(t, accs):
            at = pl.ds(pl.multiple_of(t * 8, 8), 8)
            shape_m = [terms[NM + a, k, at, :] for a in range(4)]
            diff, normal = [], [terms[NV + c, k, at, :] for c in range(3)]
            for c in range(3):
                position = shape_m[0] * corner[4 * c]
                for a in range(1, 4):
                    position = position + shape_m[a] * corner[4 * c + a]
                diff.append(position - terms[PT + c, k, at, :])
            gap = normal[0] * diff[0] + normal[1] * diff[1] + normal[2] * diff[2]
            slip = [diff[c] - normal[c] * gap for c in range(3)]
            weighted = [terms[WS + i, k, at, :] for i in range(4)]
            out = [accs[i] + weighted[i] * gap for i in range(4)]
            out += [accs[4 + c * 4 + i] + weighted[i] * slip[c] for c in range(3) for i in range(4)]
            return tuple(out)

        zero = jnp.zeros((8, LANES), jnp.float32)
        accs = lax.fori_loop(0, LANES // 8, add, (zero,) * 16, unroll=2)
        sums = [jnp.sum(acc, axis=0, keepdims=True) for acc in accs]
        cols = slice(k * LANES, (k + 1) * LANES)
        live = lane[0:1] < count_ref[0:1, k : k + 1]
        wgap = jnp.concatenate(sums[0:4], axis=0)
        active = active_ref[:, cols] == 1
        normal = nmult_ref[:, cols]
        tangent = [tmult_ref[4 * c : 4 * c + 4, cols] for c in range(3)]
        trial = [
            tangent[c] + newton_scale * jnp.concatenate(sums[4 + 4 * c : 8 + 4 * c], axis=0)
            for c in range(3)
        ]
        radius = friction_coef * normal
        length = jnp.sqrt(trial[0] * trial[0] + trial[1] * trial[1] + trial[2] * trial[2])
        factor = radius / jnp.maximum(radius, length)
        for c in range(3):
            cone = jnp.where(active, tangent[c] - factor * trial[c], tangent[c])
            cone_ref[4 * c : 4 * c + 4, cols] = jnp.where(live, cone, 0.0)
        gap_ref[:, cols] = jnp.where(live, jnp.where(active, wgap, normal), 0.0)

    sent = req_out.at[pl.ds(0, count - 1)]
    pltpu.make_async_copy(sent, sent, req_send).wait()
    sent = rep_out.at[pl.ds(0, count - 1)]
    pltpu.make_async_copy(sent, sent, rep_send).wait()


def deliver(*refs):
    sources, targets, sem = refs[:5], refs[5:10], refs[10]
    copies = [
        pltpu.make_async_copy(source, target, sem.at[at])
        for at, (source, target) in enumerate(zip(sources, targets))
    ]
    for copy in copies:
        copy.start()
    for copy in copies:
        copy.wait()


def local(
    quad_weight,
    param_coords,
    slave_points,
    slave_normals,
    block_owner,
    block_patch,
    block_count,
    active_flags,
    normal_mult,
    tangent_mult,
    master_patch,
):
    zones, peers = lax.axis_size("zone"), lax.axis_size("dev")
    slots, gauss = quad_weight.shape
    block = slots // zones
    patches = master_patch.shape[1]
    count = zones * peers
    f32 = jnp.float32
    hbm = pl.BlockSpec(memory_space=pltpu.HBM)
    vmem = pl.BlockSpec(memory_space=pltpu.VMEM)
    out = [jax.ShapeDtypeStruct((rows, slots), f32) for rows in (16, 16, 48, 4, 12)]
    results = pl.pallas_call(
        functools.partial(kernel, zones, peers),
        out_shape=out,
        in_specs=[hbm] * 11,
        out_specs=[vmem] * 5,
        scratch_shapes=[
            pltpu.VMEM((slots, gauss), f32),
            pltpu.VMEM((4 * slots, gauss), f32),
            pltpu.VMEM((3, slots, gauss), f32),
            pltpu.VMEM((3, slots, gauss), f32),
            pltpu.VMEM((12, patches), f32),
            pltpu.VMEM((8, patches // 2), f32),
            pltpu.VMEM((zones, block), jnp.int32),
            pltpu.VMEM((zones, block), jnp.int32),
            pltpu.VMEM((1, zones), jnp.int32),
            pltpu.VMEM((4, slots), jnp.int32),
            pltpu.VMEM((4, slots), f32),
            pltpu.VMEM((12, slots), f32),
            pltpu.VMEM((18, zones, gauss, block), f32),
            pltpu.VMEM((count, 1, LANES), jnp.int32),
            pltpu.VMEM((count, 1, LANES), jnp.int32),
            pltpu.VMEM((count, 1, 2 * LANES), f32),
            pltpu.VMEM((count, 1, 2 * LANES), f32),
            pltpu.SemaphoreType.DMA((11,)),
            pltpu.SemaphoreType.DMA,
            pltpu.SemaphoreType.DMA((zones,)),
            pltpu.SemaphoreType.DMA,
            pltpu.SemaphoreType.DMA((zones,)),
        ],
        compiler_params=pltpu.CompilerParams(
            collective_id=0, has_side_effects=True
        ),
    )(
        quad_weight,
        param_coords.reshape(4 * slots, gauss),
        slave_points.transpose(1, 0, 2),
        slave_normals.transpose(1, 0, 2),
        master_patch,
        block_owner.reshape(zones, block),
        block_patch.reshape(zones, block),
        block_count,
        active_flags,
        normal_mult,
        tangent_mult,
    )
    return pl.pallas_call(
        deliver,
        out_shape=out,
        in_specs=[vmem] * 5,
        out_specs=[hbm] * 5,
        scratch_shapes=[pltpu.SemaphoreType.DMA((5,))],
    )(*results)


def solution(mesh):
    rows = P(("zone", "dev"))
    columns = P(None, ("zone", "dev"))
    return jax.shard_map(
        local,
        mesh=mesh,
        in_specs=(rows,) * 7 + (columns,) * 4,
        out_specs=(columns,) * 5,
        check_vma=False,
    )
```

```python
import functools

import jax
import jax.numpy as jnp
from jax import lax
from jax.experimental import pallas as pl
from jax.experimental.pallas import tpu as pltpu
from jax.sharding import PartitionSpec as P

BUCKET = 16
LANES = 128
MESH = pl.DeviceIdType.MESH

friction_coef = 0.3
newton_scale = 4.0


def pick(values, index, axis):
    return jnp.take_along_axis(values, index, axis=axis, mode="promise_in_bounds")


def iota(shape, axis):
    return lax.broadcasted_iota(jnp.int32, shape, axis)


def bilinear(first, second):
    return (
        0.25 * (1.0 - first) * (1.0 - second),
        0.25 * (1.0 + first) * (1.0 - second),
        0.25 * (1.0 + first) * (1.0 + second),
        0.25 * (1.0 - first) * (1.0 + second),
    )


NS, NM, WS, PT, NV = 0, 4, 8, 12, 15


def kernel(
    zones,
    peers,
    quad_hbm,
    coords_hbm,
    points_hbm,
    normals_hbm,
    master_hbm,
    owner_hbm,
    patch_hbm,
    count_hbm,
    active_hbm,
    nmult_hbm,
    tmult_hbm,
    d_ref,
    m_ref,
    lin_ref,
    gap_ref,
    cone_ref,
    quad,
    coords,
    points,
    normals,
    table,
    packed,
    owner_ref,
    patch_ref,
    count_ref,
    active_ref,
    nmult_ref,
    tmult_ref,
    rank_ref,
    terms,
    req_out,
    req_in,
    rep_out,
    rep_in,
    load_sem,
    req_send,
    req_recv,
    rep_send,
    rep_recv,
):
    count = zones * peers
    groups = peers // 8
    zone, dev = lax.axis_index("zone"), lax.axis_index("dev")
    me = zone * peers + dev
    tiles = table.shape[1] // LANES
    half = tiles // 2

    barrier = pltpu.get_barrier_semaphore()

    def greet(step, carry):
        other = lax.rem(me + step, count)
        pl.semaphore_signal(
            barrier,
            inc=1,
            device_id=(lax.div(other, peers), lax.rem(other, peers)),
            device_id_type=MESH,
        )
        return carry

    lax.fori_loop(1, count, greet, 0)

    loads = [
        pltpu.make_async_copy(source, target, load_sem.at[at])
        for at, (source, target) in enumerate(
            (
                (owner_hbm, owner_ref),
                (patch_hbm, patch_ref),
                (master_hbm, table),
                (quad_hbm, quad),
                (coords_hbm, coords),
                (points_hbm, points),
                (normals_hbm, normals),
                (count_hbm, count_ref),
                (active_hbm, active_ref),
                (nmult_hbm, nmult_ref),
                (tmult_hbm, tmult_ref),
            )
        )
    ]
    for load in loads:
        load.start()

    sub, lane = iota((8, LANES), 0), iota((8, LANES), 1)
    wide_sub, wide_lane = iota((LANES, LANES), 0), iota((LANES, LANES), 1)
    loads[0].wait()
    loads[1].wait()
    for k in range(zones):
        owner = owner_ref[k : k + 1, :].astype(jnp.float32)
        patch = patch_ref[k : k + 1, :].astype(jnp.float32)
        across = jnp.broadcast_to(owner, (LANES, LANES))
        same = (across.T == across) & (wide_sub < wide_lane)
        rank = jnp.sum(jnp.where(same, 1.0, 0.0), axis=0, keepdims=True).astype(jnp.int32)
        rank_ref[k : k + 1, :] = rank
        place = owner_ref[k : k + 1, :] * BUCKET + rank
        for g in range(groups):
            chosen = jnp.where(wide_sub + g * LANES == place, jnp.broadcast_to(patch, (LANES, LANES)), 0.0)
            asked = jnp.sum(chosen.T, axis=0, keepdims=True).astype(jnp.int32)
            rows = pick(jnp.broadcast_to(asked, (8, LANES)), sub * BUCKET + (lane & 15), 1)
            for o in range(8):
                req_out[k * peers + g * 8 + o] = rows[o : o + 1, :]

    pl.semaphore_wait(barrier, count - 1)

    for dz in range(zones):
        target = lax.rem(zone - dz + zones, zones)

        def ask(step, carry):
            peer = lax.rem(dev + step, peers)
            pltpu.make_async_remote_copy(
                src_ref=req_out.at[target * peers + peer],
                dst_ref=req_in.at[me],
                send_sem=req_send,
                recv_sem=req_recv.at[zone],
                device_id=(target, peer),
                device_id_type=MESH,
            ).start()
            return carry

        if dz == 0:
            pltpu.make_async_copy(req_out.at[me], req_in.at[me], req_recv.at[zone]).start()
        lax.fori_loop(1 if dz == 0 else 0, peers, ask, 0)

    loads[2].wait()
    packed[0:4, :] = table[8:12, 0 : half * LANES]
    packed[4:8, :] = table[8:12, half * LANES : tiles * LANES]
    for load in loads[3:]:
        load.wait()

    def stage(k, carry):
        rows = pl.ds(pl.multiple_of(k * LANES, LANES), LANES)

        def coord(which):
            return coords[pl.ds(k * (4 * LANES) + which, LANES, stride=4), :].T

        weight = quad[rows, :].T
        shape_s = bilinear(coord(2), coord(3))
        for i in range(4):
            terms[NS + i, k] = shape_s[i]
            terms[WS + i, k] = weight * shape_s[i]
        shape_m = bilinear(coord(0), coord(1))
        for i in range(4):
            terms[NM + i, k] = shape_m[i]
        for c in range(3):
            terms[PT + c, k] = points[c, rows, :].T
            terms[NV + c, k] = normals[c, rows, :].T
        return carry

    lax.fori_loop(0, zones, stage, 0)

    skew = ((lane >> 4) - sub) & 7
    skew_low = ((lane >> 4) - (sub & 3)) & 7
    upper = jnp.where(sub >= 4, half, 0)
    for dz in range(zones):
        target = lax.rem(zone + dz, zones)
        whole = req_in.at[pl.ds(target * peers, peers)]
        pltpu.make_async_copy(whole, whole, req_recv.at[target]).wait()
        for g in range(groups):
            base = target * peers + g * 8
            rows = jnp.concatenate([req_in[base + v] for v in range(8)], axis=0)
            first = pick(rows, skew, 0)
            second = pick(rows, skew_low, 0)
            high, low = first >> 7, first & 127
            high_b, low_b = (second >> 7) - upper, second & 127
            zero = jnp.zeros((8, LANES), jnp.float32)

            def search(h, accs):
                acc, acc_a, acc_b = accs
                at = pl.ds(pl.multiple_of(h * LANES, LANES), LANES)
                later = pl.ds(pl.multiple_of((h + half) * LANES, LANES), LANES)
                acc = jnp.where(high == h, pick(table[0:8, at], low, 1), acc)
                acc_a = jnp.where(high == h + half, pick(table[0:8, later], low, 1), acc_a)
                acc_b = jnp.where(high_b == h, pick(packed[:, at], low_b, 1), acc_b)
                return acc, acc_a, acc_b

            acc, acc_a, acc_b = lax.fori_loop(0, half, search, (zero, zero, zero), unroll=8)
            acc = jnp.where(high >= half, acc_a, acc)
            acc_b = acc_b + pltpu.roll(acc_b, 4, 0)
            out_a, out_b = pick(acc, skew, 0), pick(acc_b, skew, 0)
            for v in range(8):
                rep_out[base + v, :, 0:LANES] = out_a[v : v + 1, :]
                rep_out[base + v, :, LANES : 2 * LANES] = out_b[v : v + 1, :]

        def answer(step, carry):
            peer = lax.rem(dev + step, peers)
            pltpu.make_async_remote_copy(
                src_ref=rep_out.at[target * peers + peer],
                dst_ref=rep_in.at[me],
                send_sem=rep_send,
                recv_sem=rep_recv.at[zone],
                device_id=(target, peer),
                device_id_type=MESH,
            ).start()
            return carry

        if dz == 0:
            pltpu.make_async_copy(rep_out.at[me], rep_in.at[me], rep_recv.at[zone]).start()
        lax.fori_loop(1 if dz == 0 else 0, peers, answer, 0)

    for k in range(zones):
        live = lane[0:1] < count_ref[0:1, k : k + 1]
        cols = slice(k * LANES, (k + 1) * LANES)

        def keep(ref, row, value):
            total = jnp.sum(value, axis=0, keepdims=True)
            ref[row : row + 1, cols] = jnp.where(live, total, 0.0)

        for i in range(4):

            def add(t, accs):
                at = pl.ds(pl.multiple_of(t * 8, 8), 8)
                weighted = terms[WS + i, k, at, :]
                normal = [terms[NV + c, k, at, :] for c in range(3)]
                out = [accs[j] + weighted * terms[NS + j, k, at, :] for j in range(4)]
                pairs = [weighted * terms[NM + a, k, at, :] for a in range(4)]
                out += [accs[4 + a] + pairs[a] for a in range(4)]
                out += [accs[8 + c * 4 + a] + pairs[a] * normal[c] for c in range(3) for a in range(4)]
                return tuple(out)

            zero = jnp.zeros((8, LANES), jnp.float32)
            accs = lax.fori_loop(0, LANES // 8, add, (zero,) * 20, unroll=4)
            for j in range(4):
                keep(d_ref, i * 4 + j, accs[j])
                keep(m_ref, i * 4 + j, accs[4 + j])
                for c in range(3):
                    keep(lin_ref, c * 16 + i * 4 + j, accs[8 + c * 4 + j])

    turn = dev & 7
    undo = ((((lane >> 4) - sub) & 7) << 4) + (lane & 15)
    mix = ((lane >> 4) - sub - turn) & 7
    for dz in range(zones):
        k = lax.rem(zone - dz + zones, zones)
        whole = rep_in.at[pl.ds(k * peers, peers)]
        pltpu.make_async_copy(whole, whole, rep_recv.at[k]).wait()
        owner = jnp.broadcast_to(owner_ref[pl.ds(k, 1), :], (8, LANES))
        seat = (((owner + sub + turn) & 7) << 4) + jnp.broadcast_to(rank_ref[pl.ds(k, 1), :], (8, LANES))
        found = []
        for h in range(2):
            total = jnp.zeros((8, LANES), jnp.float32)
            for g in range(groups):
                rows = jnp.concatenate(
                    [
                        rep_in[k * peers + g * 8 + o, :, h * LANES : (h + 1) * LANES]
                        for o in range(8)
                    ],
                    axis=0,
                )
                rows = pick(pick(pick(rows, undo, 1), mix, 0), seat, 1)
                total = jnp.where((owner >> 3) == g, rows, total)
            found.append(total)
        corner = [
            jnp.broadcast_to(found[r // 8][r % 8 : r % 8 + 1, :], (8, LANES)) for r in range(12)
        ]

        def add(t, accs):
            at = pl.ds(pl.multiple_of(t * 8, 8), 8)
            shape_m = [terms[NM + a, k, at, :] for a in range(4)]
            diff, normal = [], [terms[NV + c, k, at, :] for c in range(3)]
            for c in range(3):
                position = shape_m[0] * corner[4 * c]
                for a in range(1, 4):
                    position = position + shape_m[a] * corner[4 * c + a]
                diff.append(position - terms[PT + c, k, at, :])
            gap = normal[0] * diff[0] + normal[1] * diff[1] + normal[2] * diff[2]
            slip = [diff[c] - normal[c] * gap for c in range(3)]
            weighted = [terms[WS + i, k, at, :] for i in range(4)]
            out = [accs[i] + weighted[i] * gap for i in range(4)]
            out += [accs[4 + c * 4 + i] + weighted[i] * slip[c] for c in range(3) for i in range(4)]
            return tuple(out)

        zero = jnp.zeros((8, LANES), jnp.float32)
        accs = lax.fori_loop(0, LANES // 8, add, (zero,) * 16, unroll=2)
        sums = [jnp.sum(acc, axis=0, keepdims=True) for acc in accs]
        cols = pl.ds(pl.multiple_of(k * LANES, LANES), LANES)
        group = jnp.where(iota((1, zones), 1) == k, count_ref[...], 0)
        live = lane[0:1] < jnp.sum(group, axis=1, keepdims=True)
        wgap = jnp.concatenate(sums[0:4], axis=0)
        active = active_ref[:, cols] == 1
        normal = nmult_ref[:, cols]
        tangent = [tmult_ref[4 * c : 4 * c + 4, cols] for c in range(3)]
        trial = [
            tangent[c] + newton_scale * jnp.concatenate(sums[4 + 4 * c : 8 + 4 * c], axis=0)
            for c in range(3)
        ]
        radius = friction_coef * normal
        length = jnp.sqrt(trial[0] * trial[0] + trial[1] * trial[1] + trial[2] * trial[2])
        factor = radius / jnp.maximum(radius, length)
        for c in range(3):
            cone = jnp.where(active, tangent[c] - factor * trial[c], tangent[c])
            cone_ref[4 * c : 4 * c + 4, cols] = jnp.where(live, cone, 0.0)
        gap_ref[:, cols] = jnp.where(live, jnp.where(active, wgap, normal), 0.0)

    sent = req_out.at[pl.ds(0, count - 1)]
    pltpu.make_async_copy(sent, sent, req_send).wait()
    sent = rep_out.at[pl.ds(0, count - 1)]
    pltpu.make_async_copy(sent, sent, rep_send).wait()


def deliver(*refs):
    sources, targets, sem = refs[:5], refs[5:10], refs[10]
    copies = [
        pltpu.make_async_copy(source, target, sem.at[at])
        for at, (source, target) in enumerate(zip(sources, targets))
    ]
    for copy in copies:
        copy.start()
    for copy in copies:
        copy.wait()


def local(
    quad_weight,
    param_coords,
    slave_points,
    slave_normals,
    block_owner,
    block_patch,
    block_count,
    active_flags,
    normal_mult,
    tangent_mult,
    master_patch,
):
    zones, peers = lax.axis_size("zone"), lax.axis_size("dev")
    slots, gauss = quad_weight.shape
    block = slots // zones
    patches = master_patch.shape[1]
    count = zones * peers
    f32 = jnp.float32
    hbm = pl.BlockSpec(memory_space=pltpu.HBM)
    vmem = pl.BlockSpec(memory_space=pltpu.VMEM)
    out = [jax.ShapeDtypeStruct((rows, slots), f32) for rows in (16, 16, 48, 4, 12)]
    results = pl.pallas_call(
        functools.partial(kernel, zones, peers),
        out_shape=out,
        in_specs=[hbm] * 11,
        out_specs=[vmem] * 5,
        scratch_shapes=[
            pltpu.VMEM((slots, gauss), f32),
            pltpu.VMEM((4 * slots, gauss), f32),
            pltpu.VMEM((3, slots, gauss), f32),
            pltpu.VMEM((3, slots, gauss), f32),
            pltpu.VMEM((12, patches), f32),
            pltpu.VMEM((8, patches // 2), f32),
            pltpu.VMEM((zones, block), jnp.int32),
            pltpu.VMEM((zones, block), jnp.int32),
            pltpu.VMEM((1, zones), jnp.int32),
            pltpu.VMEM((4, slots), jnp.int32),
            pltpu.VMEM((4, slots), f32),
            pltpu.VMEM((12, slots), f32),
            pltpu.VMEM((zones, block), jnp.int32),
            pltpu.VMEM((18, zones, gauss, block), f32),
            pltpu.VMEM((count, 1, LANES), jnp.int32),
            pltpu.VMEM((count, 1, LANES), jnp.int32),
            pltpu.VMEM((count, 1, 2 * LANES), f32),
            pltpu.VMEM((count, 1, 2 * LANES), f32),
            pltpu.SemaphoreType.DMA((11,)),
            pltpu.SemaphoreType.DMA,
            pltpu.SemaphoreType.DMA((zones,)),
            pltpu.SemaphoreType.DMA,
            pltpu.SemaphoreType.DMA((zones,)),
        ],
        compiler_params=pltpu.CompilerParams(
            collective_id=0, has_side_effects=True, vmem_limit_bytes=36 * 2**20
        ),
    )(*[pltpu.with_memory_space_constraint(x, pltpu.HBM) for x in (
        quad_weight,
        param_coords.reshape(4 * slots, gauss),
        slave_points.transpose(1, 0, 2),
        slave_normals.transpose(1, 0, 2),
        master_patch,
        block_owner.reshape(zones, block),
        block_patch.reshape(zones, block),
        block_count,
        active_flags,
        normal_mult,
        tangent_mult,
    )])
    return pl.pallas_call(
        deliver,
        out_shape=out,
        in_specs=[vmem] * 5,
        out_specs=[hbm] * 5,
        scratch_shapes=[pltpu.SemaphoreType.DMA((5,))],
        compiler_params=pltpu.CompilerParams(vmem_limit_bytes=8 * 2**20),
    )(*results)


def solution(mesh):
    rows = P(("zone", "dev"))
    columns = P(None, ("zone", "dev"))
    return jax.shard_map(
        local,
        mesh=mesh,
        in_specs=(rows,) * 7 + (columns,) * 4,
        out_specs=(columns,) * 5,
        check_vma=False,
    )
```
